128 devices in a mesh: row: 16 (over x_hi, y, core), col: 8 (over z, x_lo).
Axes of the slice: x: 4 (x_hi: 2, x_lo: 2; x = x_hi * 2 + x_lo), y: 4, z: 4, core: 2. Of those that a mesh axis runs over, the one named last changes fastest.
Arguments:
- values: float32 [8192, 8192], P('row', 'col'), may hold values from 0 to 10, as said below
- pattern: int32 [64, 64], replicated, may hold values from 0 to 1, as said below
- pruning: int32 [64, 64], replicated, may hold values from 0 to 1, as said below
- owners: int32 [64], replicated, may hold values from 0 to 63, as said below
Outputs:
- expanded: float32 [8192, 8192], P('row', 'col')
The draws below stay inside these ranges and needn't reach their ends.
Inputs may be any that keep to these rules, and one draw needn't show every extreme that they name: `values`: positive scores. `pattern`: every diagonal block is present. `pruning`: every diagonal block is kept. `owners`: A permutation of the 64 column blocks. Of the 8 column blocks of one index of col, at most 2 are stored at the column blocks of any one index of col, and exactly 2 at those of some index.
All inputs are finite; a program needn't handle non-finite values.
Results may differ from the reference program's by a relative error of at most 0.00065.
Values may be sent and summed in bfloat16 or wider, within the bound.
No kernel may reach another device: no remote copies, remote signals or barrier semaphores. Data moves between devices by JAX's collectives and lax.ppermute only.
A program may use at most 128 MiB of HBM per device.

```python
import math
import jax
import jax.numpy as jnp
from jax import lax

NBLK = 64
NODES = 8192
CBD = 8
CAP = 2


def draw_values(key, part):
    key_base = jax.random.fold_in(key, 0)
    rows_pos = jnp.arange(NODES, dtype=jnp.float32)
    ramp = 1.0 + 2.0 * rows_pos / (NODES - 1)
    base = jnp.exp(jax.random.uniform(key_base, (NODES, NODES), jnp.float32, math.log(0.05), 0.0))
    return base * ramp[:, None]


def block_bits(key):
    bits = jax.random.randint(key, (NBLK, NBLK), 0, 2)
    diagonal = jnp.arange(NBLK)[:, None] == jnp.arange(NBLK)[None, :]
    return jnp.where(diagonal, 1, bits).astype(jnp.int32)


def draw_pattern(key, part):
    return block_bits(jax.random.fold_in(key, 11))


def draw_pruning(key, part):
    return block_bits(jax.random.fold_in(key, 23))


def draw_owners(key, part):
    ncols = NBLK // CBD
    key_order, key_turn, key_slot = jax.random.split(jax.random.fold_in(key, 37), 3)
    items = ncols * CAP
    scores = jax.random.permutation(key_order, items).astype(jnp.int32)
    item_ids = jnp.arange(items, dtype=jnp.int32)
    scores = jnp.where(item_ids < CAP, item_ids - CAP, scores)
    ordered = jnp.argsort(scores)
    residue = (ordered[:CBD] // CAP).astype(jnp.int32)
    turn = jax.random.randint(key_turn, (), 0, ncols).astype(jnp.int32)
    shifts = (residue + turn) % ncols
    slots = jax.random.permutation(key_slot, CBD).astype(jnp.int32)
    source = jnp.arange(NBLK, dtype=jnp.int32) // CBD
    within = jnp.arange(NBLK, dtype=jnp.int32) % CBD
    return ((source + shifts[within]) % ncols * CBD + slots[within]).astype(jnp.int32)


def setup_inputs(seed: int = 0) -> dict:
    key_of = jax.random.split(jax.random.key(seed), 5)
    values = draw_values(jax.random.fold_in(key_of[4], 71), 0)
    pattern = draw_pattern(jax.random.fold_in(key_of[4], 71), 0)
    pruning = draw_pruning(jax.random.fold_in(key_of[4], 71), 0)
    owners = draw_owners(jax.random.fold_in(key_of[4], 71), 0)
    return {"values": values, "pattern": pattern, "pruning": pruning, "owners": owners}


def expand_mask(tile, mask, blk):
    rows_in, cols_in = tile.shape
    shaped = tile.reshape(rows_in // blk, blk, cols_in // blk, blk)
    return (shaped * mask.astype(tile.dtype)[:, None, :, None]).reshape(rows_in, cols_in)


def reference(values, pattern, pruning, owners):
    nodes = values.shape[0]
    nblocks = pattern.shape[0]
    blk = nodes // nblocks
    masked = expand_mask(values, pattern, blk)
    colsum_in = jnp.sum(masked, axis=0)
    stochastic = (masked / colsum_in[None, :]).astype(jnp.bfloat16)
    widened = stochastic.astype(jnp.float32)
    square = jnp.dot(widened, widened, precision=lax.Precision.HIGHEST, preferred_element_type=jnp.float32)
    inflated = expand_mask(square * square, pruning, blk)
    colsum_out = jnp.sum(inflated, axis=0)
    normalized = NODES * inflated / colsum_out[None, :]
    column_blocks = normalized.reshape(nodes, nblocks, blk)
    placed = jnp.zeros_like(column_blocks).at[:, owners].set(column_blocks)
    return placed.reshape(nodes, nodes)
```

```python
import jax
import jax.numpy as jnp
from jax import lax
from jax.experimental import pallas as pl
from jax.experimental.pallas import tpu as pltpu
from jax.sharding import PartitionSpec as P

BLK = 128
ROWS = 512
COLS = 1024
NC = 8
NR = 16
CAP = 2
AXES = ("row", "col")


def decode(i):
    r, c = divmod(i, NC)
    return {"xh": r >> 3, "y": (r >> 1) & 3, "t": r & 1, "z": c >> 1, "xl": c & 1}


def encode(d):
    return ((d["xh"] << 3) | (d["y"] << 1) | d["t"]) * NC + ((d["z"] << 1) | d["xl"])


def flip(axis):
    out = []
    for i in range(NR * NC):
        d = decode(i)
        d[axis] ^= 1
        out.append((i, encode(d)))
    return out


def spread(axis):
    out = []
    for i in range(NR * NC):
        d = decode(i)
        d[axis] = (d[axis] + (1 if d["t"] == 0 else -1)) % 4
        out.append((i, encode(d)))
    return out


def send(x, pairs):
    return lax.ppermute(x, AXES, pairs)


def mask_kernel(keep_ref, v_ref, m_ref, p_ref):
    i = pl.program_id(0)

    @pl.when(i == 0)
    def _():
        p_ref[...] = jnp.zeros_like(p_ref)

    for j in range(COLS // BLK):
        sl = pl.ds(j * BLK, BLK)
        v = v_ref[:, sl]
        v = jnp.where(keep_ref[i, j] != 0, v, jnp.zeros_like(v))
        m_ref[:, sl] = v.astype(jnp.bfloat16)
        p_ref[:, sl] += jnp.sum(v.reshape(BLK // 8, 8, BLK), axis=0)


def mask_and_sum(values, keep):
    return pl.pallas_call(
        mask_kernel,
        grid_spec=pltpu.PrefetchScalarGridSpec(
            num_scalar_prefetch=1,
            grid=(ROWS // BLK,),
            in_specs=[pl.BlockSpec((BLK, COLS), lambda i, k: (i, 0))],
            out_specs=[
                pl.BlockSpec((BLK, COLS), lambda i, k: (i, 0)),
                pl.BlockSpec((8, COLS), lambda i, k: (0, 0)),
            ],
        ),
        out_shape=[
            jax.ShapeDtypeStruct((ROWS, COLS), jnp.bfloat16),
            jax.ShapeDtypeStruct((8, COLS), jnp.float32),
        ],
    )(keep, values)


def square_kernel(meta, keep, inv_ref, *refs):
    a_refs, b_refs = refs[:8], refs[8:20]
    g_ref, p_ref = refs[20:22]
    a_buf, b_buf, acc, a_sem, b_sem = refs[22:]
    xh, y, t, z, xl = (meta[i] for i in range(5))
    step = 2 * t - 1
    copies_a = []
    for i, (dz, dx) in enumerate(
        [(0, 0), (step, 0), (-step, 0), (2, 0), (0, 1), (step, 1), (-step, 1), (2, 1)]
    ):
        c = ((z + dz) & 3) * 2 + (xl ^ dx)
        src = a_refs[i]
        src = src.at[pl.ds(0, ROWS)] if src.shape[0] != ROWS else src
        copies_a.append(pltpu.make_async_copy(src, a_buf.at[c], a_sem.at[i]))
    copies_b = []
    order = []
    lo, hi = t * ROWS, (1 - t) * ROWS
    for dxh in range(2):
        own, other, q, qo, f, fo = b_refs[6 * dxh : 6 * dxh + 6]
        base = (xh ^ dxh) * 4
        c0, cs = base + y, base + ((y + step) & 3)
        cm, c2 = base + ((y - step) & 3), base + ((y + 2) & 3)
        first, second = pl.ds(0, ROWS), pl.ds(ROWS, ROWS)
        for c, pieces in (
            (c0, ((own, lo), (other, hi))),
            (cs, ((q.at[first], lo), (q.at[second], hi))),
            (cm, ((qo.at[first], hi), (qo.at[second], lo))),
            (c2, ((f, lo), (fo, hi))),
        ):
            group = []
            for src, at in pieces:
                k = len(copies_b)
                copy = pltpu.make_async_copy(
                    src, b_buf.at[c, pl.ds(pl.multiple_of(at, ROWS), ROWS)], b_sem.at[k]
                )
                copies_b.append(copy)
                group.append(copy)
            order.append((c, group))
    for copy in copies_a:
        copy.start()
    for copy in copies_b:
        copy.start()
    for copy in copies_a:
        copy.wait()
    for n, (c, group) in enumerate(order):
        for copy in group:
            copy.wait()
        a = (a_buf[c].astype(jnp.float32) * inv_ref[pl.ds(c, 1), :]).astype(jnp.bfloat16)
        part = jnp.dot(a, b_buf[c], preferred_element_type=jnp.float32)
        if n == 0:
            acc[...] = part
        else:
            acc[...] += part
    scale = inv_ref[pl.ds(z * 2 + xl, 1), :]
    for j in range(COLS // BLK):
        sl = pl.ds(j * BLK, BLK)
        total = jnp.zeros((8, BLK), jnp.float32)
        for i in range(ROWS // BLK):
            rows = pl.ds(i * BLK, BLK)
            g = acc[rows, sl] * scale[:, j * BLK : (j + 1) * BLK]
            g = jnp.where(keep[i * NC + j] != 0, g * g, jnp.zeros_like(g))
            g_ref[rows, sl] = g
            total += jnp.sum(g.reshape(BLK // 8, 8, BLK), axis=0)
        p_ref[:, sl] = total


def square_of(meta, keep, inv, a_pieces, b_pieces):
    anywhere = pl.BlockSpec(memory_space=pl.ANY)
    smem = pl.BlockSpec(memory_space=pltpu.SMEM)
    return pl.pallas_call(
        square_kernel,
        in_specs=[smem, smem, pl.BlockSpec(memory_space=pltpu.VMEM)] + [anywhere] * 20,
        out_specs=[pl.BlockSpec(memory_space=pltpu.VMEM)] * 2,
        out_shape=[
            jax.ShapeDtypeStruct((ROWS, COLS), jnp.float32),
            jax.ShapeDtypeStruct((8, COLS), jnp.float32),
        ],
        scratch_shapes=[
            pltpu.VMEM((NC, ROWS, COLS), jnp.bfloat16),
            pltpu.VMEM((NC, 2 * ROWS, COLS), jnp.bfloat16),
            pltpu.VMEM((ROWS, COLS), jnp.float32),
            pltpu.SemaphoreType.DMA((8,)),
            pltpu.SemaphoreType.DMA((16,)),
        ],
    )(meta, keep, inv, *a_pieces, *b_pieces)


def pack_kernel(index, g_ref, n_ref, o_ref):
    o_ref[0] = g_ref[...] * n_ref[...]


def pack_blocks(inflated, norm, index):
    n = NC * CAP
    return pl.pallas_call(
        pack_kernel,
        grid_spec=pltpu.PrefetchScalarGridSpec(
            num_scalar_prefetch=1,
            grid=(n,),
            in_specs=[
                pl.BlockSpec((ROWS, BLK), lambda i, k: (0, k[i])),
                pl.BlockSpec((1, BLK), lambda i, k: (0, k[i])),
            ],
            out_specs=pl.BlockSpec((1, ROWS, BLK), lambda i, k: (i, 0, 0)),
        ),
        out_shape=jax.ShapeDtypeStruct((n, ROWS, BLK), jnp.float32),
    )(index, inflated, norm)


def unpack_kernel(index, a_ref, o_ref):
    o_ref[...] = a_ref[0]


def unpack_blocks(arrived, index):
    return pl.pallas_call(
        unpack_kernel,
        grid_spec=pltpu.PrefetchScalarGridSpec(
            num_scalar_prefetch=1,
            grid=(NC,),
            in_specs=[pl.BlockSpec((1, ROWS, BLK), lambda i, k: (k[i], 0, 0))],
            out_specs=pl.BlockSpec((ROWS, BLK), lambda i, k: (0, i)),
        ),
        out_shape=jax.ShapeDtypeStruct((ROWS, COLS), jnp.float32),
    )(index, arrived)


def slot_tables(owners, me_col):
    table = owners.reshape(NC, NC)
    dest = table // NC
    earlier = jnp.arange(NC)[:, None] < jnp.arange(NC)[None, :]
    same = dest[:, :, None] == dest[:, None, :]
    rank = jnp.sum(jnp.where(same & earlier, 1, 0), axis=1)
    slots = jnp.arange(NC * CAP)
    mine = lax.dynamic_slice(dest, (me_col, 0), (1, NC))[0]
    my_rank = lax.dynamic_slice(rank, (me_col, 0), (1, NC))[0]
    hit = (mine[None, :] * CAP + my_rank[None, :]) == slots[:, None]
    outgoing = jnp.sum(jnp.where(hit, jnp.arange(NC)[None, :], 0), axis=1)
    slot_of = jnp.arange(NC)[:, None] * CAP + rank
    wanted = me_col * NC + jnp.arange(NC)
    match = table[None] == wanted[:, None, None]
    incoming = jnp.sum(jnp.where(match, slot_of[None], 0), axis=(1, 2))
    return outgoing.astype(jnp.int32), incoming.astype(jnp.int32)


def row_sum(p):
    v = jnp.sum(p, axis=0).reshape(1, 8, BLK)
    every = lax.all_to_all(jnp.broadcast_to(v, (NR, 8, BLK)), "row", 0, 0, tiled=True)
    return jnp.sum(every, axis=0)


def body(values, pattern, pruning, owners):
    me_row = lax.axis_index("row").astype(jnp.int32)
    me_col = lax.axis_index("col").astype(jnp.int32)
    meta = jnp.stack([me_row >> 3, (me_row >> 1) & 3, me_row & 1, me_col >> 1, me_col & 1])
    nb = ROWS // BLK
    present = lax.dynamic_slice(pattern, (me_row * nb, me_col * NC), (nb, NC))
    keep = lax.dynamic_slice(pruning, (me_row * nb, me_col * NC), (nb, NC)).reshape(nb * NC)
    m, p = mask_and_sum(values, present)

    core, ring_z, ring_y = flip("t"), spread("z"), spread("y")
    f = send(m, flip("xl"))
    h = send(m, flip("xh"))
    m_o = send(m, core)
    pair = jnp.concatenate([m, m_o], axis=0)
    rz = send(pair, ring_z)
    ry = send(pair, ring_y)
    d = row_sum(p)
    inv = lax.all_to_all(jnp.broadcast_to((1.0 / d)[None], (NC, 8, BLK)), "col", 0, 0, tiled=True)
    inv = inv.reshape(NC, COLS)
    f_o = send(f, core)
    rfz = send(jnp.concatenate([f, f_o], axis=0), ring_z)
    h_o = send(h, core)
    rhy = send(jnp.concatenate([h, h_o], axis=0), ring_y)
    qz = send(rz[:ROWS], ring_z)
    qy = send(ry[:ROWS], ring_y)
    qfz = send(rfz[:ROWS], ring_z)
    qhy = send(rhy[:ROWS], ring_y)
    a_pieces = [m, rz, send(rz[ROWS:], core), qz, f, rfz, send(rfz[ROWS:], core), qfz]
    b_pieces = [m, m_o, ry, send(ry, core), qy, send(qy, core)]
    b_pieces += [h, h_o, rhy, send(rhy, core), qhy, send(qhy, core)]
    inflated, p_out = square_of(meta, keep, inv, a_pieces, b_pieces)

    outgoing, incoming = slot_tables(owners, me_col)
    norm = jnp.float32(NR * ROWS) / row_sum(p_out).reshape(1, COLS)
    slots = pack_blocks(inflated, norm, outgoing).astype(jnp.float16)
    arrived = lax.all_to_all(slots, "col", 0, 0, tiled=True)
    return unpack_blocks(arrived.astype(jnp.float32), incoming)


def solution(mesh):
    return jax.shard_map(
        body,
        mesh=mesh,
        in_specs=(P("row", "col"), P(), P(), P()),
        out_specs=P("row", "col"),
        check_vma=False,
    )
```

```python
import jax
import jax.numpy as jnp
from jax import lax
from jax.experimental import pallas as pl
from jax.experimental.pallas import tpu as pltpu
from jax.sharding import PartitionSpec as P


BLK = 128
ROWS = 512
COLS = 1024
NC = 8
NR = 16
CAP = 2
AXES = ("row", "col")


def decode(i):
    r, c = divmod(i, NC)
    return {"xh": r >> 3, "y": (r >> 1) & 3, "t": r & 1, "z": c >> 1, "xl": c & 1}


def encode(d):
    return ((d["xh"] << 3) | (d["y"] << 1) | d["t"]) * NC + ((d["z"] << 1) | d["xl"])


def flip(axis):
    out = []
    for i in range(NR * NC):
        d = decode(i)
        d[axis] ^= 1
        out.append((i, encode(d)))
    return out


def spread(axis):
    out = []
    for i in range(NR * NC):
        d = decode(i)
        d[axis] = (d[axis] + (1 if d["t"] == 0 else -1)) % 4
        out.append((i, encode(d)))
    return out


def send(x, pairs):
    return lax.ppermute(x, AXES, pairs)


def mask_kernel(keep_ref, v_ref, m_ref, ma_ref, mb_ref, p_ref):
    i = pl.program_id(0)

    @pl.when(i == 0)
    def _():
        p_ref[...] = jnp.zeros_like(p_ref)

    for j in range(COLS // BLK):
        sl = pl.ds(j * BLK, BLK)
        v = v_ref[:, sl]
        v = jnp.where(keep_ref[i, j] != 0, v, jnp.zeros_like(v))
        m = v.astype(jnp.bfloat16)
        m_ref[:, sl] = m

        @pl.when(i < 2)
        def _():
            ma_ref[:, sl] = m

        @pl.when(i >= 2)
        def _():
            mb_ref[:, sl] = m

        p_ref[:, sl] += jnp.sum(v.reshape(BLK // 8, 8, BLK), axis=0)


def mask_and_sum(values, keep):
    return pl.pallas_call(
        mask_kernel,
        grid_spec=pltpu.PrefetchScalarGridSpec(
            num_scalar_prefetch=1,
            grid=(ROWS // BLK,),
            in_specs=[pl.BlockSpec((BLK, COLS), lambda i, k: (i, 0))],
            out_specs=[
                pl.BlockSpec((BLK, COLS), lambda i, k: (i, 0)),
                pl.BlockSpec((BLK, COLS), lambda i, k: (jnp.minimum(i, 1), 0)),
                pl.BlockSpec((BLK, COLS), lambda i, k: (jnp.maximum(i, 2) - 2, 0)),
                pl.BlockSpec((8, COLS), lambda i, k: (0, 0)),
            ],
        ),
        out_shape=[
            jax.ShapeDtypeStruct((ROWS, COLS), jnp.bfloat16),
            jax.ShapeDtypeStruct((ROWS // 2, COLS), jnp.bfloat16),
            jax.ShapeDtypeStruct((ROWS // 2, COLS), jnp.bfloat16),
            jax.ShapeDtypeStruct((8, COLS), jnp.float32),
        ],
    )(keep, values)


def square_kernel(meta, keep, inv_ref, *refs):
    a_refs, b_refs = refs[:8], refs[8:24]
    h_ref, p_ref = refs[24:26]
    a_buf, b_buf, acc, a_sem, b_sem = refs[26:]
    xh, y, t, z, xl = (meta[i] for i in range(5))
    step = 2 * t - 1
    copies_a = []
    for i in range(8):
        dz = (0, step, -step, 2)[i % 4]
        c = ((z + dz) & 3) * 2 + (xl ^ (i // 4))
        copies_a.append(pltpu.make_async_copy(a_refs[i], a_buf.at[c], a_sem.at[i]))
    lo, hi = pl.multiple_of(t * ROWS, ROWS), pl.multiple_of((1 - t) * ROWS, ROWS)
    order = []
    for i in range(8):
        dy = (0, step, -step, 2)[i % 4]
        c = (xh ^ (i // 4)) * 4 + ((y + dy) & 3)
        group = []
        for k, at in ((2 * i, lo), (2 * i + 1, hi)):
            dst = b_buf.at[c, pl.ds(at, ROWS)]
            group.append(pltpu.make_async_copy(b_refs[k], dst, b_sem.at[k]))
        order.append((c, group))
    for copy in copies_a:
        copy.start()
    for _, group in order:
        for copy in group:
            copy.start()
    for copy in copies_a:
        copy.wait()
    for n, (c, group) in enumerate(order):
        for copy in group:
            copy.wait()
        a = (a_buf[c].astype(jnp.float32) * inv_ref[pl.ds(c, 1), :]).astype(jnp.bfloat16)
        part = jnp.dot(a, b_buf[c], preferred_element_type=jnp.float32)
        if n == 0:
            acc[...] = part
        else:
            acc[...] += part
    scale = inv_ref[pl.ds(z * 2 + xl, 1), :]
    for j in range(NC):
        sl = pl.ds(j * BLK, BLK)
        total = jnp.zeros((8, BLK), jnp.float32)
        for i in range(ROWS // BLK):
            rows = pl.ds(i * BLK, BLK)
            g = acc[rows, sl] * scale[:, j * BLK : (j + 1) * BLK]
            g = jnp.where(keep[i * NC + j] != 0, g * g, jnp.zeros_like(g))
            h_ref[j, rows] = g
            total += jnp.sum(g.reshape(BLK // 8, 8, BLK), axis=0)
        p_ref[pl.ds(j, 1), :] = jnp.sum(total, axis=0, keepdims=True)


def square_of(meta, keep, inv, a_pieces, b_pieces):
    anywhere = pl.BlockSpec(memory_space=pl.ANY)
    smem = pl.BlockSpec(memory_space=pltpu.SMEM)
    return pl.pallas_call(
        square_kernel,
        in_specs=[smem, smem, pl.BlockSpec(memory_space=pltpu.VMEM)] + [anywhere] * 24,
        out_specs=[pl.BlockSpec(memory_space=pltpu.VMEM)] * 2,
        out_shape=[
            jax.ShapeDtypeStruct((NC, ROWS, BLK), jnp.float32),
            jax.ShapeDtypeStruct((NC, BLK), jnp.float32),
        ],
        scratch_shapes=[
            pltpu.VMEM((NC, ROWS, COLS), jnp.bfloat16),
            pltpu.VMEM((NC, 2 * ROWS, COLS), jnp.bfloat16),
            pltpu.VMEM((ROWS, COLS), jnp.float32),
            pltpu.SemaphoreType.DMA((8,)),
            pltpu.SemaphoreType.DMA((16,)),
        ],
    )(meta, keep, inv, *a_pieces, *b_pieces)


def slot_tables(owners, me_col):
    table = owners.reshape(NC, NC)
    dest = table // NC
    earlier = jnp.arange(NC)[:, None] < jnp.arange(NC)[None, :]
    same = dest[:, :, None] == dest[:, None, :]
    rank = jnp.sum(jnp.where(same & earlier, 1, 0), axis=1)
    slots = jnp.arange(NC * CAP)
    mine = lax.dynamic_slice(dest, (me_col, 0), (1, NC))[0]
    my_rank = lax.dynamic_slice(rank, (me_col, 0), (1, NC))[0]
    hit = (mine[None, :] * CAP + my_rank[None, :]) == slots[:, None]
    outgoing = jnp.sum(jnp.where(hit, jnp.arange(NC)[None, :], 0), axis=1)
    slot_of = jnp.arange(NC)[:, None] * CAP + rank
    wanted = me_col * NC + jnp.arange(NC)
    match = table[None] == wanted[:, None, None]
    incoming = jnp.sum(jnp.where(match, slot_of[None], 0), axis=(1, 2))
    return outgoing.astype(jnp.int32), incoming.astype(jnp.int32)


def row_sum(v):
    every = lax.all_to_all(jnp.broadcast_to(v[None], (NR, NC, BLK)), "row", 0, 0, tiled=True)
    return jnp.sum(every, axis=0)


def body(values, pattern, pruning, owners):
    me_row = lax.axis_index("row").astype(jnp.int32)
    me_col = lax.axis_index("col").astype(jnp.int32)
    meta = jnp.stack([me_row >> 3, (me_row >> 1) & 3, me_row & 1, me_col >> 1, me_col & 1])
    nb = ROWS // BLK
    present = lax.dynamic_slice(pattern, (me_row * nb, me_col * NC), (nb, NC))
    keep = lax.dynamic_slice(pruning, (me_row * nb, me_col * NC), (nb, NC)).reshape(nb * NC)
    outgoing, incoming = slot_tables(owners, me_col)
    m, ma, mb, p = mask_and_sum(values, present)
    p = jnp.sum(p, axis=0).reshape(NC, BLK)

    core, ring_z, ring_y = flip("t"), spread("z"), spread("y")

    def swap(x):
        return send(x, core)

    ha = send(ma, flip("xh"))
    yu = send(m, ring_y)
    mo = send(m, core)
    d = row_sum(p)
    zu = send(m, ring_z)
    fa = send(ma, flip("xl"))
    yv = send(mo, ring_y)
    zv = send(mo, ring_z)
    hb = send(mb, flip("xh"))
    fb = send(mb, flip("xl"))
    yuu = send(yu, ring_y)
    zuu = send(zu, ring_z)
    inv = jnp.broadcast_to((1.0 / d)[None], (NC, NC, BLK))
    inv = lax.all_to_all(inv, "col", 0, 0, tiled=True).reshape(NC, COLS)
    h = jnp.concatenate([ha, hb], axis=0)
    yh = send(h, ring_y)
    ho = send(h, core)
    yho = send(ho, ring_y)
    f = jnp.concatenate([fa, fb], axis=0)
    zf = send(f, ring_z)
    fo = send(f, core)
    zfo = send(fo, ring_z)
    xzz = send(zuu, flip("xl"))
    yhh = send(yh, ring_y)
    a_pieces = [m, zu, swap(zv), zuu, f, zf, swap(zfo), xzz]
    b_pieces = [m, mo, yu, yv, swap(yv), swap(yu), yuu, swap(yuu)]
    b_pieces += [h, ho, yh, yho, swap(yho), swap(yh), yhh, swap(yhh)]
    inflated, p_out = square_of(meta, keep, inv, a_pieces, b_pieces)
    norm = jnp.float32(NR * ROWS) / row_sum(p_out)
    half = (inflated * norm[:, None, :]).astype(jnp.float16)
    slots = jnp.take(half, outgoing, axis=0, mode="clip")
    arrived = lax.all_to_all(slots, "col", 0, 0, tiled=True)
    placed = jnp.take(arrived, incoming, axis=0, mode="clip").astype(jnp.float32)
    return placed.transpose(1, 0, 2).reshape(ROWS, COLS)


def solution(mesh):
    return jax.shard_map(
        body,
        mesh=mesh,
        in_specs=(P("row", "col"), P(), P(), P()),
        out_specs=P("row", "col"),
        check_vma=False,
    )
```

```python
import jax
import jax.numpy as jnp
from jax import lax
from jax.experimental import pallas as pl
from jax.experimental.pallas import tpu as pltpu
from jax.sharding import PartitionSpec as P


BLK = 128
ROWS = 512
COLS = 1024
NC = 8
NR = 16
CAP = 2
EARLY_LIMIT = 4 << 20
LATE_LIMIT = 19 << 20
AXES = ("row", "col")


def decode(i):
    r, c = divmod(i, NC)
    return {"xh": r >> 3, "y": (r >> 1) & 3, "t": r & 1, "z": c >> 1, "xl": c & 1}


def encode(d):
    return ((d["xh"] << 3) | (d["y"] << 1) | d["t"]) * NC + ((d["z"] << 1) | d["xl"])


def flip(axis):
    out = []
    for i in range(NR * NC):
        d = decode(i)
        d[axis] ^= 1
        out.append((i, encode(d)))
    return out


def spread(axis):
    out = []
    for i in range(NR * NC):
        d = decode(i)
        d[axis] = (d[axis] + (1 if d["t"] == 0 else -1)) % 4
        out.append((i, encode(d)))
    return out


def ring_xor(bit):
    out = []
    for i in range(NR * NC):
        d = decode(i)
        d["y"] ^= bit
        out.append((i, encode(d)))
    return out


def send(x, pairs):
    return lax.ppermute(x, AXES, pairs)


def mask_kernel(keep_ref, v_ref, m_ref, ma_ref, mb_ref, p_ref):
    i = pl.program_id(0)

    @pl.when(i == 0)
    def _():
        p_ref[...] = jnp.zeros_like(p_ref)

    for j in range(COLS // BLK):
        sl = pl.ds(j * BLK, BLK)
        v = v_ref[:, sl]
        v = jnp.where(keep_ref[i, j] != 0, v, jnp.zeros_like(v))
        m = v.astype(jnp.bfloat16)
        m_ref[:, sl] = m

        @pl.when(i < 2)
        def _():
            ma_ref[:, sl] = m

        @pl.when(i >= 2)
        def _():
            mb_ref[:, sl] = m

        p_ref[:, sl] += jnp.sum(v.reshape(BLK // 8, 8, BLK), axis=0)


def mask_and_sum(values, keep):
    return pl.pallas_call(
        mask_kernel,
        grid_spec=pltpu.PrefetchScalarGridSpec(
            num_scalar_prefetch=1,
            grid=(ROWS // BLK,),
            in_specs=[pl.BlockSpec((BLK, COLS), lambda i, k: (i, 0))],
            out_specs=[
                pl.BlockSpec((BLK, COLS), lambda i, k: (i, 0)),
                pl.BlockSpec((BLK, COLS), lambda i, k: (jnp.minimum(i, 1), 0)),
                pl.BlockSpec((BLK, COLS), lambda i, k: (jnp.maximum(i, 2) - 2, 0)),
                pl.BlockSpec((8, COLS), lambda i, k: (0, 0)),
            ],
        ),
        out_shape=[
            jax.ShapeDtypeStruct((ROWS, COLS), jnp.bfloat16),
            jax.ShapeDtypeStruct((ROWS // 2, COLS), jnp.bfloat16),
            jax.ShapeDtypeStruct((ROWS // 2, COLS), jnp.bfloat16),
            jax.ShapeDtypeStruct((8, COLS), jnp.float32),
        ],
    )(keep, values)


def early_kernel(meta, keep, outgoing, incoming, inv_ref, *refs):
    del keep, outgoing, incoming
    a_refs, b_refs = refs[:4], refs[4:12]
    a_buf, b_buf, acc, sem = refs[12:]
    xh, y, t, z, xl = (meta[i] for i in range(5))
    copies = panel_copies(t, z, y, [[r] for r in a_refs], b_refs, a_buf, b_buf, sem)
    for copy in copies[0] + copies[1]:
        copy.start()
    for copy in copies[0] + copies[1]:
        copy.wait()
    for k in range(2):
        part = block_product(inv_ref, a_buf, b_buf, xh, xl + 2 * k)
        if k == 0:
            acc[...] = part
        else:
            acc[...] += part


def panel_copies(t, z, y, a_pieces, b_pieces, a_buf, b_buf, sem):
    step = 2 * t - 1
    lo, hi = pl.multiple_of(t * ROWS, ROWS), pl.multiple_of((1 - t) * ROWS, ROWS)
    first, second = [], []
    for i in range(4):
        d = (0, step, -step, 2)[i]
        at = 0
        for ref in a_pieces[i]:
            rows = ref.shape[0]
            n = len(first)
            dst = a_buf.at[(z + d) & 3, pl.ds(at, rows)]
            first.append(pltpu.make_async_copy(ref, dst, sem.at[n]))
            at += rows
        for k, at in ((2 * i, lo), (2 * i + 1, hi)):
            dst = b_buf.at[(y + d) & 3, pl.ds(at, ROWS)]
            second.append(pltpu.make_async_copy(b_pieces[k], dst, sem.at[8 + k]))
    return first, second


def block_product(inv_ref, a_buf, b_buf, xh, y):
    scale = inv_ref[pl.ds(xh * 4 + y, 1), :]
    a = (a_buf[xh * 2 + (y >> 1)].astype(jnp.float32) * scale).astype(jnp.bfloat16)
    return jnp.dot(a, b_buf[y], preferred_element_type=jnp.float32)


def early_product(meta, tables, inv, a_pieces, b_pieces):
    anywhere = pl.BlockSpec(memory_space=pltpu.HBM)
    smem = pl.BlockSpec(memory_space=pltpu.SMEM)
    vmem = pl.BlockSpec(memory_space=pltpu.VMEM)
    out = pl.pallas_call(
        early_kernel,
        in_specs=[smem] * 4 + [vmem] + [anywhere] * 12,
        out_specs=[vmem] * 3,
        out_shape=[
            jax.ShapeDtypeStruct((4, ROWS, COLS), jnp.bfloat16),
            jax.ShapeDtypeStruct((4, 2 * ROWS, COLS), jnp.bfloat16),
            jax.ShapeDtypeStruct((ROWS, COLS), jnp.float32),
        ],
        scratch_shapes=[pltpu.SemaphoreType.DMA((16,))],
        compiler_params=pltpu.CompilerParams(vmem_limit_bytes=EARLY_LIMIT),
    )(meta, *tables, inv, *a_pieces, *b_pieces)
    return [pltpu.with_memory_space_constraint(x, pltpu.VMEM) for x in out]


def late_kernel(meta, keep, inv_ref, ae_ref, be_ref, part_ref, *refs):
    a_refs, b_refs = refs[:7], refs[7:15]
    h_ref, p_ref = refs[15:17]
    a_buf, b_buf, acc, sem = refs[17:]
    xh, y, t, z, xl = (meta[i] for i in range(5))
    pieces = [a_refs[0:2], a_refs[2:4], a_refs[4:6], a_refs[6:7]]
    first, second = panel_copies(t, z, y, pieces, b_refs, a_buf, b_buf, sem)
    for copy in first + second:
        copy.start()
    for copy in first:
        copy.wait()
    acc[...] = part_ref[...]
    for k in range(2):
        acc[...] += block_product(inv_ref, a_buf, be_ref, xh, (1 - xl) + 2 * k)
    for copy in second:
        copy.wait()
    for k in range(2):
        acc[...] += block_product(inv_ref, ae_ref, b_buf, 1 - xh, xl + 2 * k)
    for k in range(2):
        acc[...] += block_product(inv_ref, a_buf, b_buf, 1 - xh, (1 - xl) + 2 * k)
    scale = inv_ref[pl.ds(z * 2 + xl, 1), :]
    for j in range(NC):
        sl = pl.ds(j * BLK, BLK)
        total = jnp.zeros((8, BLK), jnp.float32)
        for i in range(ROWS // BLK):
            rows = pl.ds(i * BLK, BLK)
            g = acc[rows, sl] * scale[:, j * BLK : (j + 1) * BLK]
            g = jnp.where(keep[i * NC + j] != 0, g * g, jnp.zeros_like(g))
            h_ref[j, rows] = g
            total += jnp.sum(g.reshape(BLK // 8, 8, BLK), axis=0)
        total = jnp.sum(total, axis=0, keepdims=True)
        p_ref[pl.ds(j, 1), :] = total
        r = jnp.where(total > 0, 1.0 / total, jnp.zeros_like(total))
        h_ref[j] = h_ref[j] * r * jnp.float32(ROWS)


def late_product(meta, keep, inv, early, a_pieces, b_pieces):
    anywhere = pl.BlockSpec(memory_space=pltpu.HBM)
    smem = pl.BlockSpec(memory_space=pltpu.SMEM)
    vmem = pl.BlockSpec(memory_space=pltpu.VMEM)
    return pl.pallas_call(
        late_kernel,
        in_specs=[smem, smem] + [vmem] * 4 + [anywhere] * 15,
        out_specs=[vmem] * 2,
        out_shape=[
            jax.ShapeDtypeStruct((NC, ROWS, BLK), jnp.float32),
            jax.ShapeDtypeStruct((NC, BLK), jnp.float32),
        ],
        scratch_shapes=[
            pltpu.VMEM((4, ROWS, COLS), jnp.bfloat16),
            pltpu.VMEM((4, 2 * ROWS, COLS), jnp.bfloat16),
            pltpu.VMEM((ROWS, COLS), jnp.float32),
            pltpu.SemaphoreType.DMA((16,)),
        ],
        compiler_params=pltpu.CompilerParams(vmem_limit_bytes=LATE_LIMIT),
    )(meta, keep, inv, *early, *a_pieces, *b_pieces)


def columns_kernel(x_ref, o_ref, sem):
    copies = []
    for j in range(NC):
        dst = o_ref.at[:, pl.ds(j * BLK, BLK)]
        copies.append(pltpu.make_async_copy(x_ref.at[j], dst, sem.at[j]))
    for copy in copies:
        copy.start()
    for copy in copies:
        copy.wait()


def side_by_side(blocks):
    return pl.pallas_call(
        columns_kernel,
        in_specs=[pl.BlockSpec(memory_space=pltpu.VMEM)],
        out_specs=pl.BlockSpec(memory_space=pltpu.HBM),
        out_shape=jax.ShapeDtypeStruct((ROWS, COLS), jnp.float32),
        scratch_shapes=[pltpu.SemaphoreType.DMA((NC,))],
        compiler_params=pltpu.CompilerParams(vmem_limit_bytes=EARLY_LIMIT),
    )(pltpu.with_memory_space_constraint(blocks, pltpu.VMEM))


def slot_tables(owners, me_col):
    table = owners.reshape(NC, NC)
    dest = table // NC
    earlier = jnp.arange(NC)[:, None] < jnp.arange(NC)[None, :]
    same = dest[:, :, None] == dest[:, None, :]
    rank = jnp.sum(jnp.where(same & earlier, 1, 0), axis=1)
    slots = jnp.arange(NC * CAP)
    mine = lax.dynamic_slice(dest, (me_col, 0), (1, NC))[0]
    my_rank = lax.dynamic_slice(rank, (me_col, 0), (1, NC))[0]
    hit = (mine[None, :] * CAP + my_rank[None, :]) == slots[:, None]
    outgoing = jnp.sum(jnp.where(hit, jnp.arange(NC)[None, :], 0), axis=1)
    slot_of = jnp.arange(NC)[:, None] * CAP + rank
    wanted = me_col * NC + jnp.arange(NC)
    match = table[None] == wanted[:, None, None]
    incoming = jnp.sum(jnp.where(match, slot_of[None], 0), axis=(1, 2))
    return outgoing.astype(jnp.int32), incoming.astype(jnp.int32)


def row_sum(v):
    every = lax.all_to_all(jnp.broadcast_to(v[None], (NR, NC, BLK)), "row", 0, 0, tiled=True)
    return jnp.sum(every, axis=0)


def body(values, pattern, pruning, owners):
    me_row = lax.axis_index("row").astype(jnp.int32)
    me_col = lax.axis_index("col").astype(jnp.int32)
    meta = jnp.stack([me_row >> 3, (me_row >> 1) & 3, me_row & 1, me_col >> 1, me_col & 1])
    nb = ROWS // BLK
    present = lax.dynamic_slice(pattern, (me_row * nb, me_col * NC), (nb, NC))
    keep = lax.dynamic_slice(pruning, (me_row * nb, me_col * NC), (nb, NC)).reshape(nb * NC)
    m, ma, mb, p = mask_and_sum(values, present)
    p = jnp.sum(p, axis=0).reshape(NC, BLK)

    core, ring_z, ring_y = flip("t"), spread("z"), spread("y")

    def swap(x):
        return send(x, core)

    outgoing, incoming = slot_tables(owners, me_col)
    h = send(m, flip("xh"))
    yu = send(m, ring_y)
    mo = send(m, core)
    d = row_sum(p)
    zu = send(m, ring_z)
    yv = send(mo, ring_y)
    zv = send(mo, ring_z)
    fa = send(ma, flip("xl"))
    fb = send(mb, flip("xl"))
    yuu = send(yu, ring_y)
    zuu = send(zu, ring_z)
    inv = jnp.broadcast_to((1.0 / d)[None], (NC, NC, BLK))
    inv = lax.all_to_all(inv, "col", 0, 0, tiled=True).reshape(NC, COLS)
    ho = send(h, core)
    yh = send(h, ring_y)
    yho = send(ho, ring_y)
    foa = send(fa, core)
    zfa = send(fa, ring_z)
    zfoa = send(foa, ring_z)
    fob = send(fb, core)
    zfb = send(fb, ring_z)
    zfob = send(fob, ring_z)
    xzz = send(zuu, flip("xl"))
    yhh = send(yh, ring_y)
    early = early_product(
        meta, (keep, outgoing, incoming), inv,
        [m, zu, swap(zv), zuu],
        [m, mo, yu, yv, swap(yv), swap(yu), yuu, swap(yuu)],
    )
    shares, p_out = late_product(
        meta, keep, inv, early,
        [fa, fb, zfa, zfb, swap(zfoa), swap(zfob), xzz],
        [h, ho, yh, yho, swap(yho), swap(yh), yhh, swap(yhh)],
    )
    sums = jnp.take(p_out, outgoing, axis=0, mode="clip")
    sums = lax.all_to_all(sums, "col", 0, 0, tiled=True)
    slots = jnp.take(shares.astype(jnp.float16), outgoing, axis=0, mode="clip")
    arrived = lax.all_to_all(slots, "col", 0, 0, tiled=True)
    sums = jnp.take(sums, incoming, axis=0, mode="clip")
    total = sums + send(sums, core)
    total = total + send(total, ring_xor(1))
    total = total + send(total, ring_xor(2))
    total = total + send(total, flip("xh"))
    weight = sums / total * jnp.float32(NR)
    placed = jnp.take(arrived, incoming, axis=0, mode="clip")
    return side_by_side(placed.astype(jnp.float32) * weight[:, None, :])


def solution(mesh):
    return jax.shard_map(
        body,
        mesh=mesh,
        in_specs=(P("row", "col"), P(), P(), P()),
        out_specs=P("row", "col"),
        check_vma=False,
    )
```

```python
import jax
import jax.numpy as jnp
from jax import lax
from jax.experimental import pallas as pl
from jax.experimental.pallas import tpu as pltpu
from jax.sharding import PartitionSpec as P


BLK = 128
ROWS = 512
COLS = 1024
NC = 8
NR = 16
CAP = 2
EARLY_LIMIT = 8 << 20
LAST_LIMIT = 4 << 20
LATE_LIMIT = 32 << 20
AXES = ("row", "col")


def decode(i):
    r, c = divmod(i, NC)
    return {"xh": r >> 3, "y": (r >> 1) & 3, "t": r & 1, "z": c >> 1, "xl": c & 1}


def encode(d):
    return ((d["xh"] << 3) | (d["y"] << 1) | d["t"]) * NC + ((d["z"] << 1) | d["xl"])


def flip(axis):
    out = []
    for i in range(NR * NC):
        d = decode(i)
        d[axis] ^= 1
        out.append((i, encode(d)))
    return out


def spread(axis):
    out = []
    for i in range(NR * NC):
        d = decode(i)
        d[axis] = (d[axis] + (1 if d["t"] == 0 else -1)) % 4
        out.append((i, encode(d)))
    return out


def ring_xor(bit):
    out = []
    for i in range(NR * NC):
        d = decode(i)
        d["y"] ^= bit
        out.append((i, encode(d)))
    return out


def send(x, pairs):
    return lax.ppermute(x, AXES, pairs)


def mask_kernel(dev, pattern_ref, v_ref, m_ref, every_ref, p_ref):
    i = pl.program_id(0)
    nb = ROWS // BLK

    @pl.when(i == 0)
    def _():
        p_ref[...] = jnp.zeros_like(p_ref)

    for j in range(NC):
        sl = pl.ds(j * BLK, BLK)
        for q in range(nb // 2):
            rows = pl.ds(q * BLK, BLK)
            present = pattern_ref[(dev[0] >> 3) * nb + i * (nb // 2) + q, (dev[0] & 7) * NC + j]
            v = v_ref[rows, sl]
            v = jnp.where(present != 0, v, jnp.zeros_like(v))
            m_ref[rows, sl] = v.astype(jnp.bfloat16)
            p_ref[:, sl] += jnp.sum(v.reshape(BLK // 8, 8, BLK), axis=0)

    @pl.when(i == 1)
    def _():
        for j in range(NC):
            total = jnp.sum(p_ref[:, pl.ds(j * BLK, BLK)], axis=0, keepdims=True)
            for k in range(NR):
                every_ref[k, pl.ds(j, 1), :] = total


def mask_and_sum(dev, pattern, values):
    return pl.pallas_call(
        mask_kernel,
        grid_spec=pltpu.PrefetchScalarGridSpec(
            num_scalar_prefetch=2,
            grid=(2,),
            in_specs=[pl.BlockSpec((ROWS // 2, COLS), lambda i, *_: (i, 0))],
            out_specs=[
                pl.BlockSpec((ROWS // 2, COLS), lambda i, *_: (i, 0)),
                pl.BlockSpec((NR, NC, BLK), lambda i, *_: (0, 0, 0)),
            ],
            scratch_shapes=[pltpu.VMEM((8, COLS), jnp.float32)],
        ),
        out_shape=[
            jax.ShapeDtypeStruct((ROWS, COLS), jnp.bfloat16),
            jax.ShapeDtypeStruct((NR, NC, BLK), jnp.float32),
        ],
    )(dev, pattern, values)


def early_kernel(meta, keep, outgoing, incoming, inv_ref, *refs):
    del keep, outgoing, incoming
    a_refs, b_refs, across = refs[:4], refs[4:12], refs[12:16]
    a_buf, b_buf, acc, third, sem = refs[16:]
    xh, y, t, z, xl = (meta[i] for i in range(5))
    copies = panel_copies(t, z, y, [[r] for r in a_refs], b_refs, a_buf, b_buf, sem)
    for copy in copies[0] + copies[1]:
        copy.start()
    lo, hi = pl.multiple_of(t * ROWS, ROWS), pl.multiple_of((1 - t) * ROWS, ROWS)
    even = ((y ^ xl) & 1) == 0
    for pred, pair in ((even, across[:2]), (jnp.logical_not(even), across[2:])):

        @pl.when(pred)
        def _(pair=pair):
            pltpu.make_async_copy(pair[0], third.at[0, pl.ds(lo, ROWS)], sem.at[16]).start()
            pltpu.make_async_copy(pair[1], third.at[0, pl.ds(hi, ROWS)], sem.at[17]).start()

    for copy in copies[0] + copies[1]:
        copy.wait()
    acc[...] = block_product(inv_ref, a_buf, b_buf, xh, xl)
    acc[...] += block_product(inv_ref, a_buf, b_buf, xh, xl + 2)
    pltpu.make_async_copy(across[0], third.at[0, pl.ds(lo, ROWS)], sem.at[16]).wait()
    pltpu.make_async_copy(across[1], third.at[0, pl.ds(hi, ROWS)], sem.at[17]).wait()
    acc[...] += block_product(inv_ref, a_buf, third, 1 - xh, third_place(t, y, xl), 0)


def third_place(t, y, xl):
    return jnp.where(((y ^ xl) & 1) == 0, y, (y + 2 * t - 1) & 3)


def panel_copies(t, z, y, a_pieces, b_pieces, a_buf, b_buf, sem):
    step = 2 * t - 1
    lo, hi = pl.multiple_of(t * ROWS, ROWS), pl.multiple_of((1 - t) * ROWS, ROWS)
    first, second = [], []
    for i in range(4):
        d = (0, step, -step, 2)[i]
        at = 0
        for ref in a_pieces[i]:
            rows = ref.shape[0]
            n = len(first)
            dst = a_buf.at[(z + d) & 3, pl.ds(at, rows)]
            first.append(pltpu.make_async_copy(ref, dst, sem.at[n]))
            at += rows
        for k, at in ((2 * i, lo), (2 * i + 1, hi)):
            dst = b_buf.at[(y + d) & 3, pl.ds(at, ROWS)]
            second.append(pltpu.make_async_copy(b_pieces[k], dst, sem.at[8 + k]))
    return first, second


def block_product(inv_ref, a_buf, b_buf, xh, y, slot=None):
    slot = y if slot is None else slot
    scale = inv_ref[pl.ds(xh * 4 + y, 1), :]
    a = (a_buf[xh * 2 + (y >> 1)].astype(jnp.float32) * scale).astype(jnp.bfloat16)
    return jnp.dot(a, b_buf[slot], preferred_element_type=jnp.float32)


def early_product(meta, tables, inv, a_pieces, b_pieces, across):
    anywhere = pl.BlockSpec(memory_space=pltpu.HBM)
    smem = pl.BlockSpec(memory_space=pltpu.SMEM)
    vmem = pl.BlockSpec(memory_space=pltpu.VMEM)
    out = pl.pallas_call(
        early_kernel,
        in_specs=[smem] * 4 + [vmem] + [anywhere] * 16,
        out_specs=[vmem] * 3,
        out_shape=[
            jax.ShapeDtypeStruct((4, ROWS, COLS), jnp.bfloat16),
            jax.ShapeDtypeStruct((4, 2 * ROWS, COLS), jnp.bfloat16),
            jax.ShapeDtypeStruct((ROWS, COLS), jnp.float32),
        ],
        scratch_shapes=[
            pltpu.VMEM((1, 2 * ROWS, COLS), jnp.bfloat16),
            pltpu.SemaphoreType.DMA((18,)),
        ],
        compiler_params=pltpu.CompilerParams(vmem_limit_bytes=EARLY_LIMIT),
    )(meta, *tables, inv, *a_pieces, *b_pieces, *across)
    return [pltpu.with_memory_space_constraint(x, pltpu.VMEM) for x in out]


def late_kernel(meta, keep, outgoing, inv_ref, ae_ref, be_ref, part_ref, *refs):
    a_refs, b_refs = refs[:7], refs[7:15]
    h_ref, slot_ref = refs[15:17]
    a_buf, b_buf, acc, p_ref, sem = refs[17:]
    xh, y, t, z, xl = (meta[i] for i in range(5))
    pieces = [a_refs[0:2], a_refs[2:4], a_refs[4:6], a_refs[6:7]]
    first, second = panel_copies(t, z, y, pieces, b_refs, a_buf, b_buf, sem)
    for copy in first + second:
        copy.start()
    for copy in first:
        copy.wait()
    acc[...] = part_ref[...]
    for k in range(2):
        acc[...] += block_product(inv_ref, a_buf, be_ref, xh, (1 - xl) + 2 * k)
    for copy in second:
        copy.wait()
    rest = (third_place(t, y, xl) + 2) & 3
    acc[...] += block_product(inv_ref, ae_ref, b_buf, 1 - xh, rest)
    for k in range(2):
        acc[...] += block_product(inv_ref, a_buf, b_buf, 1 - xh, (1 - xl) + 2 * k)
    scale = inv_ref[pl.ds(z * 2 + xl, 1), :]
    for j in range(NC):
        sl = pl.ds(j * BLK, BLK)
        total = jnp.zeros((8, BLK), jnp.float32)
        for i in range(ROWS // BLK):
            rows = pl.ds(i * BLK, BLK)
            g = acc[rows, sl] * scale[:, j * BLK : (j + 1) * BLK]
            g = jnp.where(keep[i * NC + j] != 0, g * g, jnp.zeros_like(g))
            h_ref[j, rows] = g
            total += jnp.sum(g.reshape(BLK // 8, 8, BLK), axis=0)
        total = jnp.sum(total, axis=0, keepdims=True)
        p_ref[pl.ds(j, 1), :] = total
        r = jnp.where(total > 0, 1.0 / total, jnp.zeros_like(total))
        h_ref[j] = h_ref[j] * r * jnp.float32(ROWS)
    for k in range(NC * CAP):
        slot_ref[pl.ds(k, 1), :] = p_ref[pl.ds(outgoing[k], 1), :]


def late_product(meta, keep, outgoing, inv, early, a_pieces, b_pieces):
    anywhere = pl.BlockSpec(memory_space=pltpu.HBM)
    smem = pl.BlockSpec(memory_space=pltpu.SMEM)
    vmem = pl.BlockSpec(memory_space=pltpu.VMEM)
    return pl.pallas_call(
        late_kernel,
        in_specs=[smem] * 3 + [vmem] * 4 + [anywhere] * 15,
        out_specs=[vmem] * 2,
        out_shape=[
            jax.ShapeDtypeStruct((NC, ROWS, BLK), jnp.float32),
            jax.ShapeDtypeStruct((NC * CAP, BLK), jnp.float32),
        ],
        scratch_shapes=[
            pltpu.VMEM((4, ROWS, COLS), jnp.bfloat16),
            pltpu.VMEM((4, 2 * ROWS, COLS), jnp.bfloat16),
            pltpu.VMEM((ROWS, COLS), jnp.float32),
            pltpu.VMEM((NC, BLK), jnp.float32),
            pltpu.SemaphoreType.DMA((16,)),
        ],
        compiler_params=pltpu.CompilerParams(vmem_limit_bytes=LATE_LIMIT),
    )(meta, keep, outgoing, inv, *early, *a_pieces, *b_pieces)


def columns_kernel(x_ref, o_ref, sem):
    copies = []
    for j in range(NC):
        dst = o_ref.at[:, pl.ds(j * BLK, BLK)]
        copies.append(pltpu.make_async_copy(x_ref.at[j], dst, sem.at[j]))
    for copy in copies:
        copy.start()
    for copy in copies:
        copy.wait()


def side_by_side(blocks):
    return pl.pallas_call(
        columns_kernel,
        in_specs=[pl.BlockSpec(memory_space=pltpu.VMEM)],
        out_specs=pl.BlockSpec(memory_space=pltpu.HBM),
        out_shape=jax.ShapeDtypeStruct((ROWS, COLS), jnp.float32),
        scratch_shapes=[pltpu.SemaphoreType.DMA((NC,))],
        compiler_params=pltpu.CompilerParams(vmem_limit_bytes=LAST_LIMIT),
    )(pltpu.with_memory_space_constraint(blocks, pltpu.VMEM))


def slot_tables(owners, me_col):
    table = owners.reshape(NC, NC)
    dest = table // NC
    earlier = jnp.arange(NC)[:, None] < jnp.arange(NC)[None, :]
    same = dest[:, :, None] == dest[:, None, :]
    rank = jnp.sum(jnp.where(same & earlier, 1, 0), axis=1)
    slots = jnp.arange(NC * CAP)
    mine = lax.dynamic_slice(dest, (me_col, 0), (1, NC))[0]
    my_rank = lax.dynamic_slice(rank, (me_col, 0), (1, NC))[0]
    hit = (mine[None, :] * CAP + my_rank[None, :]) == slots[:, None]
    outgoing = jnp.sum(jnp.where(hit, jnp.arange(NC)[None, :], 0), axis=1)
    slot_of = jnp.arange(NC)[:, None] * CAP + rank
    wanted = me_col * NC + jnp.arange(NC)
    match = table[None] == wanted[:, None, None]
    incoming = jnp.sum(jnp.where(match, slot_of[None], 0), axis=(1, 2))
    return outgoing.astype(jnp.int32), incoming.astype(jnp.int32)


def body(values, pattern, pruning, owners):
    me_row = lax.axis_index("row").astype(jnp.int32)
    me_col = lax.axis_index("col").astype(jnp.int32)
    meta = jnp.stack([me_row >> 3, (me_row >> 1) & 3, me_row & 1, me_col >> 1, me_col & 1])
    nb = ROWS // BLK
    m, every = mask_and_sum((me_row * NC + me_col).reshape(1), pattern, values)

    core, ring_z, ring_y = flip("t"), spread("z"), spread("y")

    def swap(x):
        return send(x, core)

    keep = lax.dynamic_slice(pruning, (me_row * nb, me_col * NC), (nb, NC))
    keep = keep.reshape(nb * NC)
    outgoing, incoming = slot_tables(owners, me_col)
    yu = send(m, ring_y)
    mo = send(m, core)
    h = send(m, flip("xh"))
    zu = send(m, ring_z)
    d = jnp.sum(lax.all_to_all(every, "row", 0, 0, tiled=True), axis=0)
    yv = send(mo, ring_y)
    zv = send(mo, ring_z)
    fa = send(m[: ROWS // 2], flip("xl"))
    fb = send(m[ROWS // 2 :], flip("xl"))
    yuu = send(yu, ring_y)
    zuu = send(zu, ring_z)
    ho = send(h, core)
    yh = send(h, ring_y)
    yho = send(ho, ring_y)
    inv = jnp.broadcast_to((1.0 / d)[None], (NC, NC, BLK))
    inv = lax.all_to_all(inv, "col", 0, 0, tiled=True).reshape(NC, COLS)
    foa = send(fa, core)
    zfa = send(fa, ring_z)
    zfoa = send(foa, ring_z)
    xzz = send(zuu, flip("xl"))
    fob = send(fb, core)
    zfb = send(fb, ring_z)
    zfob = send(fob, ring_z)
    yhh = send(yh, ring_y)
    szfoa = send(zfoa, core)
    early = early_product(
        meta, (keep, outgoing, incoming), inv,
        [m, zu, swap(zv), zuu],
        [m, mo, yu, yv, swap(yv), swap(yu), yuu, swap(yuu)],
        [h, ho, yh, yho],
    )
    shares, sums = late_product(
        meta, keep, outgoing, inv, early,
        [fa, fb, zfa, zfb, szfoa, swap(zfob), xzz],
        [h, ho, yh, yho, swap(yho), swap(yh), yhh, swap(yhh)],
    )
    sums = lax.all_to_all(sums, "col", 0, 0, tiled=True)
    slots = jnp.take(shares.astype(jnp.float16), outgoing, axis=0, mode="clip")
    arrived = lax.all_to_all(slots, "col", 0, 0, tiled=True)
    sums = jnp.take(sums, incoming, axis=0, mode="clip")
    total = sums + send(sums, core)
    total = total + send(total, ring_xor(1))
    total = total + send(total, ring_xor(2))
    total = total + send(total, flip("xh"))
    weight = sums / total * jnp.float32(NR)
    placed = jnp.take(arrived, incoming, axis=0, mode="clip")
    return side_by_side(placed.astype(jnp.float32) * weight[:, None, :])


def solution(mesh):
    return jax.shard_map(
        body,
        mesh=mesh,
        in_specs=(P("row", "col"), P(), P(), P()),
        out_specs=P("row", "col"),
        check_vma=False,
    )
```

```python
import jax
import jax.numpy as jnp
from jax import lax
from jax.experimental import pallas as pl
from jax.experimental.pallas import tpu as pltpu
from jax.sharding import PartitionSpec as P


BLK = 128
ROWS = 512
COLS = 1024
NC = 8
NR = 16
CAP = 2
EARLY_LIMIT = 8 << 20
LAST_LIMIT = 4 << 20
LATE_LIMIT = 19 << 20
AXES = ("row", "col")


def decode(i):
    r, c = divmod(i, NC)
    return {"xh": r >> 3, "y": (r >> 1) & 3, "t": r & 1, "z": c >> 1, "xl": c & 1}


def encode(d):
    return ((d["xh"] << 3) | (d["y"] << 1) | d["t"]) * NC + ((d["z"] << 1) | d["xl"])


def flip(axis):
    out = []
    for i in range(NR * NC):
        d = decode(i)
        d[axis] ^= 1
        out.append((i, encode(d)))
    return out


def spread(axis):
    out = []
    for i in range(NR * NC):
        d = decode(i)
        d[axis] = (d[axis] + (1 if d["t"] == 0 else -1)) % 4
        out.append((i, encode(d)))
    return out


def ring_xor(bit):
    out = []
    for i in range(NR * NC):
        d = decode(i)
        d["y"] ^= bit
        out.append((i, encode(d)))
    return out


def send(x, pairs):
    return lax.ppermute(x, AXES, pairs)


def mask_kernel(dev, pattern_ref, v_ref, m_ref, every_ref, p_ref):
    i = pl.program_id(0)
    nb = ROWS // BLK

    @pl.when(i == 0)
    def _():
        p_ref[...] = jnp.zeros_like(p_ref)

    for j in range(NC):
        sl = pl.ds(j * BLK, BLK)
        for q in range(nb // 2):
            rows = pl.ds(q * BLK, BLK)
            present = pattern_ref[(dev[0] >> 3) * nb + i * (nb // 2) + q, (dev[0] & 7) * NC + j]
            v = v_ref[rows, sl]
            v = jnp.where(present != 0, v, jnp.zeros_like(v))
            m_ref[rows, sl] = v.astype(jnp.bfloat16)
            p_ref[:, sl] += jnp.sum(v.reshape(BLK // 8, 8, BLK), axis=0)

    @pl.when(i == 1)
    def _():
        for j in range(NC):
            total = jnp.sum(p_ref[:, pl.ds(j * BLK, BLK)], axis=0, keepdims=True)
            for k in range(NR):
                every_ref[k, pl.ds(j, 1), :] = total


def mask_and_sum(dev, pattern, values):
    return pl.pallas_call(
        mask_kernel,
        grid_spec=pltpu.PrefetchScalarGridSpec(
            num_scalar_prefetch=2,
            grid=(2,),
            in_specs=[pl.BlockSpec((ROWS // 2, COLS), lambda i, *_: (i, 0))],
            out_specs=[
                pl.BlockSpec((ROWS // 2, COLS), lambda i, *_: (i, 0)),
                pl.BlockSpec((NR, NC, BLK), lambda i, *_: (0, 0, 0)),
            ],
            scratch_shapes=[pltpu.VMEM((8, COLS), jnp.float32)],
        ),
        out_shape=[
            jax.ShapeDtypeStruct((ROWS, COLS), jnp.bfloat16),
            jax.ShapeDtypeStruct((NR, NC, BLK), jnp.float32),
        ],
    )(dev, pattern, values)


def early_kernel(meta, keep, outgoing, incoming, inv_ref, *refs):
    del keep, outgoing, incoming
    a_refs, b_refs, across = refs[:4], refs[4:12], refs[12:16]
    a_buf, b_buf, acc, third, sem = refs[16:]
    xh, y, t, z, xl = (meta[i] for i in range(5))
    copies = panel_copies(t, z, y, [[r] for r in a_refs], b_refs, a_buf, b_buf, sem)
    for copy in copies[0] + copies[1]:
        copy.start()
    lo, hi = pl.multiple_of(t * ROWS, ROWS), pl.multiple_of((1 - t) * ROWS, ROWS)
    even = ((y ^ xl) & 1) == 0
    for pred, pair in ((even, across[:2]), (jnp.logical_not(even), across[2:])):

        @pl.when(pred)
        def _(pair=pair):
            pltpu.make_async_copy(pair[0], third.at[0, pl.ds(lo, ROWS)], sem.at[16]).start()
            pltpu.make_async_copy(pair[1], third.at[0, pl.ds(hi, ROWS)], sem.at[17]).start()

    for copy in copies[0] + copies[1]:
        copy.wait()
    acc[...] = block_product(inv_ref, a_buf, b_buf, xh, xl)
    acc[...] += block_product(inv_ref, a_buf, b_buf, xh, xl + 2)
    pltpu.make_async_copy(across[0], third.at[0, pl.ds(lo, ROWS)], sem.at[16]).wait()
    pltpu.make_async_copy(across[1], third.at[0, pl.ds(hi, ROWS)], sem.at[17]).wait()
    acc[...] += block_product(inv_ref, a_buf, third, 1 - xh, third_place(t, y, xl), 0)


def third_place(t, y, xl):
    return jnp.where(((y ^ xl) & 1) == 0, y, (y + 2 * t - 1) & 3)


def panel_copies(t, z, y, a_pieces, b_pieces, a_buf, b_buf, sem):
    step = 2 * t - 1
    lo, hi = pl.multiple_of(t * ROWS, ROWS), pl.multiple_of((1 - t) * ROWS, ROWS)
    first, second = [], []
    for i in range(4):
        d = (0, step, -step, 2)[i]
        at = 0
        for ref in a_pieces[i]:
            rows = ref.shape[0]
            n = len(first)
            dst = a_buf.at[(z + d) & 3, pl.ds(at, rows)]
            first.append(pltpu.make_async_copy(ref, dst, sem.at[n]))
            at += rows
        for k, at in ((2 * i, lo), (2 * i + 1, hi)):
            dst = b_buf.at[(y + d) & 3, pl.ds(at, ROWS)]
            second.append(pltpu.make_async_copy(b_pieces[k], dst, sem.at[8 + k]))
    return first, second


def block_product(inv_ref, a_buf, b_buf, xh, y, slot=None):
    slot = y if slot is None else slot
    scale = inv_ref[pl.ds(xh * 4 + y, 1), :]
    a = (a_buf[xh * 2 + (y >> 1)].astype(jnp.float32) * scale).astype(jnp.bfloat16)
    return jnp.dot(a, b_buf[slot], preferred_element_type=jnp.float32)


def early_product(meta, tables, inv, a_pieces, b_pieces, across):
    anywhere = pl.BlockSpec(memory_space=pltpu.HBM)
    smem = pl.BlockSpec(memory_space=pltpu.SMEM)
    vmem = pl.BlockSpec(memory_space=pltpu.VMEM)
    out = pl.pallas_call(
        early_kernel,
        in_specs=[smem] * 4 + [vmem] + [anywhere] * 16,
        out_specs=[vmem] * 3,
        out_shape=[
            jax.ShapeDtypeStruct((4, ROWS, COLS), jnp.bfloat16),
            jax.ShapeDtypeStruct((4, 2 * ROWS, COLS), jnp.bfloat16),
            jax.ShapeDtypeStruct((ROWS, COLS), jnp.float32),
        ],
        scratch_shapes=[
            pltpu.VMEM((1, 2 * ROWS, COLS), jnp.bfloat16),
            pltpu.SemaphoreType.DMA((18,)),
        ],
        compiler_params=pltpu.CompilerParams(vmem_limit_bytes=EARLY_LIMIT),
    )(meta, *tables, inv, *a_pieces, *b_pieces, *across)
    return [pltpu.with_memory_space_constraint(x, pltpu.VMEM) for x in out]


def late_kernel(meta, keep, slots, inv_ref, ae_ref, be_ref, part_ref, *refs):
    a_refs, b_refs = refs[:7], refs[7:15]
    h_ref, slot_ref = refs[15:17]
    a_buf, b_buf, acc, sem = refs[17:]
    xh, y, t, z, xl = (meta[i] for i in range(5))
    pieces = [a_refs[0:2], a_refs[2:4], a_refs[4:6], a_refs[6:7]]
    first, second = panel_copies(t, z, y, pieces, b_refs, a_buf, b_buf, sem)
    even = ((y ^ xl) & 1) == 0
    for copy in first:
        copy.start()
    for n, pred in ((0, jnp.logical_not(even)), (1, even)):

        @pl.when(pred)
        def _(pair=second[2 * n : 2 * n + 2]):
            for copy in pair:
                copy.start()

    for copy in second[4:]:
        copy.start()
    for k in range(NC * CAP):
        h_ref[k] = jnp.zeros((ROWS, BLK), jnp.float32)
    for copy in first:
        copy.wait()
    acc[...] = part_ref[...]
    for k in range(2):
        acc[...] += block_product(inv_ref, a_buf, be_ref, xh, (1 - xl) + 2 * k)
    for n, pred in ((0, jnp.logical_not(even)), (1, even)):

        @pl.when(pred)
        def _(pair=second[2 * n : 2 * n + 2]):
            for copy in pair:
                copy.wait()

    for copy in second[4:]:
        copy.wait()
    rest = (third_place(t, y, xl) + 2) & 3
    acc[...] += block_product(inv_ref, ae_ref, b_buf, 1 - xh, rest)
    for k in range(2):
        acc[...] += block_product(inv_ref, a_buf, b_buf, 1 - xh, (1 - xl) + 2 * k)
    scale = inv_ref[pl.ds(z * 2 + xl, 1), :]
    slot_ref[...] = jnp.zeros_like(slot_ref)
    for j in range(NC):
        sl = pl.ds(j * BLK, BLK)
        slot = slots[j]
        total = jnp.zeros((8, BLK), jnp.float32)
        for i in range(ROWS // BLK):
            rows = pl.ds(i * BLK, BLK)
            g = acc[rows, sl] * scale[:, j * BLK : (j + 1) * BLK]
            g = jnp.where(keep[i * NC + j] != 0, g * g, jnp.zeros_like(g))
            acc[rows, sl] = g
            total += jnp.sum(g.reshape(BLK // 8, 8, BLK), axis=0)
        total = jnp.sum(total, axis=0, keepdims=True)
        slot_ref[pl.ds(slot, 1), :] = total
        r = jnp.where(total > 0, 1.0 / total, jnp.zeros_like(total))
        h_ref[slot] = acc[:, sl] * r * jnp.float32(ROWS)


def late_product(meta, keep, slots, inv, early, a_pieces, b_pieces):
    anywhere = pl.BlockSpec(memory_space=pltpu.HBM)
    smem = pl.BlockSpec(memory_space=pltpu.SMEM)
    vmem = pl.BlockSpec(memory_space=pltpu.VMEM)
    return pl.pallas_call(
        late_kernel,
        in_specs=[smem] * 3 + [vmem] * 4 + [anywhere] * 15,
        out_specs=[vmem] * 2,
        out_shape=[
            jax.ShapeDtypeStruct((NC * CAP, ROWS, BLK), jnp.float32),
            jax.ShapeDtypeStruct((NC * CAP, BLK), jnp.float32),
        ],
        scratch_shapes=[
            pltpu.VMEM((4, ROWS, COLS), jnp.bfloat16),
            pltpu.VMEM((4, 2 * ROWS, COLS), jnp.bfloat16),
            pltpu.VMEM((ROWS, COLS), jnp.float32),
            pltpu.SemaphoreType.DMA((16,)),
        ],
        compiler_params=pltpu.CompilerParams(vmem_limit_bytes=LATE_LIMIT),
    )(meta, keep, slots, inv, *early, *a_pieces, *b_pieces)


def columns_kernel(x_ref, o_ref, sem):
    copies = []
    for j in range(NC):
        dst = o_ref.at[:, pl.ds(j * BLK, BLK)]
        copies.append(pltpu.make_async_copy(x_ref.at[j], dst, sem.at[j]))
    for copy in copies:
        copy.start()
    for copy in copies:
        copy.wait()


def side_by_side(blocks):
    return pl.pallas_call(
        columns_kernel,
        in_specs=[pl.BlockSpec(memory_space=pltpu.VMEM)],
        out_specs=pl.BlockSpec(memory_space=pltpu.HBM),
        out_shape=jax.ShapeDtypeStruct((ROWS, COLS), jnp.float32),
        scratch_shapes=[pltpu.SemaphoreType.DMA((NC,))],
        compiler_params=pltpu.CompilerParams(vmem_limit_bytes=LAST_LIMIT),
    )(pltpu.with_memory_space_constraint(blocks, pltpu.VMEM))


def slot_tables(owners, me_col):
    table = owners.reshape(NC, NC)
    dest = table // NC
    earlier = jnp.arange(NC)[:, None] < jnp.arange(NC)[None, :]
    same = dest[:, :, None] == dest[:, None, :]
    rank = jnp.sum(jnp.where(same & earlier, 1, 0), axis=1)
    mine = lax.dynamic_slice(dest, (me_col, 0), (1, NC))[0]
    my_rank = lax.dynamic_slice(rank, (me_col, 0), (1, NC))[0]
    outgoing = mine * CAP + my_rank
    slot_of = jnp.arange(NC)[:, None] * CAP + rank
    wanted = me_col * NC + jnp.arange(NC)
    match = table[None] == wanted[:, None, None]
    incoming = jnp.sum(jnp.where(match, slot_of[None], 0), axis=(1, 2))
    return outgoing.astype(jnp.int32), incoming.astype(jnp.int32)


def body(values, pattern, pruning, owners):
    me_row = lax.axis_index("row").astype(jnp.int32)
    me_col = lax.axis_index("col").astype(jnp.int32)
    meta = jnp.stack([me_row >> 3, (me_row >> 1) & 3, me_row & 1, me_col >> 1, me_col & 1])
    nb = ROWS // BLK
    m, every = mask_and_sum((me_row * NC + me_col).reshape(1), pattern, values)

    core, ring_z, ring_y = flip("t"), spread("z"), spread("y")

    def swap(x):
        return send(x, core)

    keep = lax.dynamic_slice(pruning, (me_row * nb, me_col * NC), (nb, NC))
    keep = keep.reshape(nb * NC)
    outgoing, incoming = slot_tables(owners, me_col)
    yu = send(m, ring_y)
    mo = send(m, core)
    h = send(m, flip("xh"))
    zu = send(m, ring_z)
    d = jnp.sum(lax.all_to_all(every, "row", 0, 0, tiled=True), axis=0)
    yv = send(mo, ring_y)
    zv = send(mo, ring_z)
    fa = send(m[: ROWS // 2], flip("xl"))
    fb = send(m[ROWS // 2 :], flip("xl"))
    yuu = send(yu, ring_y)
    zuu = send(zu, ring_z)
    ho = send(h, core)
    yh = send(h, ring_y)
    yho = send(ho, ring_y)
    inv = jnp.broadcast_to((1.0 / d)[None], (NC, NC, BLK))
    inv = lax.all_to_all(inv, "col", 0, 0, tiled=True).reshape(NC, COLS)
    foa = send(fa, core)
    zfa = send(fa, ring_z)
    zfoa = send(foa, ring_z)
    xzz = send(zuu, flip("xl"))
    fob = send(fb, core)
    zfb = send(fb, ring_z)
    zfob = send(fob, ring_z)
    yhh = send(yh, ring_y)
    szfoa = send(zfoa, core)
    early = early_product(
        meta, (keep, outgoing, incoming), inv,
        [m, zu, swap(zv), zuu],
        [m, mo, yu, yv, swap(yv), swap(yu), yuu, swap(yuu)],
        [h, ho, yh, yho],
    )
    shares, sums = late_product(
        meta, keep, outgoing, inv, early,
        [fa, fb, zfa, zfb, szfoa, swap(zfob), xzz],
        [h, ho, yh, yho, swap(yho), swap(yh), yhh, swap(yhh)],
    )
    slots, sums = lax.optimization_barrier((shares.astype(jnp.float16), sums))
    sums = lax.all_to_all(sums, "col", 0, 0, tiled=True)
    arrived = lax.all_to_all(slots, "col", 0, 0, tiled=True)
    sums = jnp.take(sums, incoming, axis=0, mode="clip")
    total = sums + send(sums, core)
    total = total + send(total, ring_xor(1))
    total = total + send(total, ring_xor(2))
    total = total + send(total, flip("xh"))
    weight = sums / total * jnp.float32(NR)
    placed = jnp.take(arrived, incoming, axis=0, mode="clip")
    return side_by_side(placed.astype(jnp.float32) * weight[:, None, :])


def solution(mesh):
    return jax.shard_map(
        body,
        mesh=mesh,
        in_specs=(P("row", "col"), P(), P(), P()),
        out_specs=P("row", "col"),
        check_vma=False,
    )
```

```python
import jax
import jax.numpy as jnp
from jax import lax
from jax.experimental import pallas as pl
from jax.experimental.pallas import tpu as pltpu
from jax.sharding import PartitionSpec as P


BLK = 128
ROWS = 512
COLS = 1024
NC = 8
NR = 16
CAP = 2
EARLY_LIMIT = 8 << 20
LAST_LIMIT = 4 << 20
LATE_LIMIT = 19 << 20
AXES = ("row", "col")


def decode(i):
    r, c = divmod(i, NC)
    return {"xh": r >> 3, "y": (r >> 1) & 3, "t": r & 1, "z": c >> 1, "xl": c & 1}


def encode(d):
    return ((d["xh"] << 3) | (d["y"] << 1) | d["t"]) * NC + ((d["z"] << 1) | d["xl"])


def flip(axis):
    out = []
    for i in range(NR * NC):
        d = decode(i)
        d[axis] ^= 1
        out.append((i, encode(d)))
    return out


def spread(axis):
    out = []
    for i in range(NR * NC):
        d = decode(i)
        d[axis] = (d[axis] + (1 if d["t"] == 0 else -1)) % 4
        out.append((i, encode(d)))
    return out


def ring_xor(bit):
    out = []
    for i in range(NR * NC):
        d = decode(i)
        d["y"] ^= bit
        out.append((i, encode(d)))
    return out


def send(x, pairs):
    return lax.ppermute(x, AXES, pairs)


def mask_kernel(dev, pattern_ref, v_ref, m_ref, every_ref, p_ref):
    i = pl.program_id(0)
    nb = ROWS // BLK

    @pl.when(i == 0)
    def _():
        p_ref[...] = jnp.zeros_like(p_ref)

    for j in range(NC):
        sl = pl.ds(j * BLK, BLK)
        for q in range(nb // 2):
            rows = pl.ds(q * BLK, BLK)
            present = pattern_ref[(dev[0] >> 3) * nb + i * (nb // 2) + q, (dev[0] & 7) * NC + j]
            v = v_ref[rows, sl]
            v = jnp.where(present != 0, v, jnp.zeros_like(v))
            m_ref[rows, sl] = v.astype(jnp.bfloat16)
            p_ref[:, sl] += jnp.sum(v.reshape(BLK // 8, 8, BLK), axis=0)

    @pl.when(i == 1)
    def _():
        for j in range(NC):
            total = jnp.sum(p_ref[:, pl.ds(j * BLK, BLK)], axis=0, keepdims=True)
            for k in range(NR):
                every_ref[k, pl.ds(j, 1), :] = total


def mask_and_sum(dev, pattern, values):
    return pl.pallas_call(
        mask_kernel,
        grid_spec=pltpu.PrefetchScalarGridSpec(
            num_scalar_prefetch=2,
            grid=(2,),
            in_specs=[pl.BlockSpec((ROWS // 2, COLS), lambda i, *_: (i, 0))],
            out_specs=[
                pl.BlockSpec((ROWS // 2, COLS), lambda i, *_: (i, 0)),
                pl.BlockSpec((NR, NC, BLK), lambda i, *_: (0, 0, 0)),
            ],
            scratch_shapes=[pltpu.VMEM((8, COLS), jnp.float32)],
        ),
        out_shape=[
            jax.ShapeDtypeStruct((ROWS, COLS), jnp.bfloat16),
            jax.ShapeDtypeStruct((NR, NC, BLK), jnp.float32),
        ],
    )(dev, pattern, values)


def early_kernel(meta, keep, outgoing, incoming, inv_ref, *refs):
    del keep, outgoing, incoming
    a_refs, b_refs, across = refs[:4], refs[4:12], refs[12:16]
    a_buf, b_buf, acc, third, sem = refs[16:]
    xh, y, t, z, xl = (meta[i] for i in range(5))
    copies = panel_copies(t, z, y, [[r] for r in a_refs], b_refs, a_buf, b_buf, sem)
    for copy in copies[0] + copies[1]:
        copy.start()
    lo, hi = pl.multiple_of(t * ROWS, ROWS), pl.multiple_of((1 - t) * ROWS, ROWS)
    even = ((y ^ xl) & 1) == 0
    for pred, pair in ((even, across[:2]), (jnp.logical_not(even), across[2:])):

        @pl.when(pred)
        def _(pair=pair):
            pltpu.make_async_copy(pair[0], third.at[0, pl.ds(lo, ROWS)], sem.at[16]).start()
            pltpu.make_async_copy(pair[1], third.at[0, pl.ds(hi, ROWS)], sem.at[17]).start()

    for copy in copies[0] + copies[1]:
        copy.wait()
    acc[...] = block_product(inv_ref, a_buf, b_buf, xh, xl)
    acc[...] += block_product(inv_ref, a_buf, b_buf, xh, xl + 2)
    pltpu.make_async_copy(across[0], third.at[0, pl.ds(lo, ROWS)], sem.at[16]).wait()
    pltpu.make_async_copy(across[1], third.at[0, pl.ds(hi, ROWS)], sem.at[17]).wait()
    acc[...] += block_product(inv_ref, a_buf, third, 1 - xh, third_place(t, y, xl), 0)


def third_place(t, y, xl):
    return jnp.where(((y ^ xl) & 1) == 0, y, (y + 2 * t - 1) & 3)


def panel_copies(t, z, y, a_pieces, b_pieces, a_buf, b_buf, sem):
    step = 2 * t - 1
    lo, hi = pl.multiple_of(t * ROWS, ROWS), pl.multiple_of((1 - t) * ROWS, ROWS)
    first, second = [], []
    for i in range(4):
        d = (0, step, -step, 2)[i]
        at = 0
        for ref in a_pieces[i]:
            rows = ref.shape[0]
            n = len(first)
            dst = a_buf.at[(z + d) & 3, pl.ds(at, rows)]
            first.append(pltpu.make_async_copy(ref, dst, sem.at[n]))
            at += rows
        for k, at in ((2 * i, lo), (2 * i + 1, hi)):
            dst = b_buf.at[(y + d) & 3, pl.ds(at, ROWS)]
            second.append(pltpu.make_async_copy(b_pieces[k], dst, sem.at[8 + k]))
    return first, second


def block_product(inv_ref, a_buf, b_buf, xh, y, slot=None):
    slot = y if slot is None else slot
    scale = inv_ref[pl.ds(xh * 4 + y, 1), :]
    a = (a_buf[xh * 2 + (y >> 1)].astype(jnp.float32) * scale).astype(jnp.bfloat16)
    return jnp.dot(a, b_buf[slot], preferred_element_type=jnp.float32)


def early_product(meta, tables, inv, a_pieces, b_pieces, across):
    anywhere = pl.BlockSpec(memory_space=pltpu.HBM)
    smem = pl.BlockSpec(memory_space=pltpu.SMEM)
    vmem = pl.BlockSpec(memory_space=pltpu.VMEM)
    out = pl.pallas_call(
        early_kernel,
        in_specs=[smem] * 4 + [vmem] + [anywhere] * 16,
        out_specs=[vmem] * 3,
        out_shape=[
            jax.ShapeDtypeStruct((4, ROWS, COLS), jnp.bfloat16),
            jax.ShapeDtypeStruct((4, 2 * ROWS, COLS), jnp.bfloat16),
            jax.ShapeDtypeStruct((ROWS, COLS), jnp.float32),
        ],
        scratch_shapes=[
            pltpu.VMEM((1, 2 * ROWS, COLS), jnp.bfloat16),
            pltpu.SemaphoreType.DMA((18,)),
        ],
        compiler_params=pltpu.CompilerParams(vmem_limit_bytes=EARLY_LIMIT),
    )(meta, *tables, inv, *a_pieces, *b_pieces, *across)
    return [pltpu.with_memory_space_constraint(x, pltpu.VMEM) for x in out]


def late_kernel(meta, keep, slots, inv_ref, ae_ref, be_ref, part_ref, *refs):
    a_refs, b_refs = refs[:7], refs[7:15]
    h_ref, slot_ref = refs[15:17]
    a_buf, b_buf, acc, sem = refs[17:]
    xh, y, t, z, xl = (meta[i] for i in range(5))
    pieces = [a_refs[0:2], a_refs[2:4], a_refs[4:6], a_refs[6:7]]
    first, second = panel_copies(t, z, y, pieces, b_refs, a_buf, b_buf, sem)
    even = ((y ^ xl) & 1) == 0
    for copy in first:
        copy.start()
    for n, pred in ((0, jnp.logical_not(even)), (1, even)):

        @pl.when(pred)
        def _(pair=second[2 * n : 2 * n + 2]):
            for copy in pair:
                copy.start()

    for copy in second[4:]:
        copy.start()
    for k in range(NC * CAP):
        h_ref[k] = jnp.zeros((ROWS, BLK), jnp.float32)
    for copy in first:
        copy.wait()
    acc[...] = part_ref[...]
    for k in range(2):
        acc[...] += block_product(inv_ref, a_buf, be_ref, xh, (1 - xl) + 2 * k)
    for n, pred in ((0, jnp.logical_not(even)), (1, even)):

        @pl.when(pred)
        def _(pair=second[2 * n : 2 * n + 2]):
            for copy in pair:
                copy.wait()

    for copy in second[4:]:
        copy.wait()
    rest = (third_place(t, y, xl) + 2) & 3
    acc[...] += block_product(inv_ref, ae_ref, b_buf, 1 - xh, rest)
    for k in range(2):
        acc[...] += block_product(inv_ref, a_buf, b_buf, 1 - xh, (1 - xl) + 2 * k)
    scale = inv_ref[pl.ds(z * 2 + xl, 1), :]
    slot_ref[...] = jnp.zeros_like(slot_ref)
    for j in range(NC):
        sl = pl.ds(j * BLK, BLK)
        slot = slots[j]
        total = jnp.zeros((8, BLK), jnp.float32)
        for i in range(ROWS // BLK):
            rows = pl.ds(i * BLK, BLK)
            g = acc[rows, sl] * scale[:, j * BLK : (j + 1) * BLK]
            g = jnp.where(keep[i * NC + j] != 0, g * g, jnp.zeros_like(g))
            acc[rows, sl] = g
            total += jnp.sum(g.reshape(BLK // 8, 8, BLK), axis=0)
        total = jnp.sum(total, axis=0, keepdims=True)
        slot_ref[pl.ds(slot, 1), :] = total
        r = jnp.where(total > 0, 1.0 / total, jnp.zeros_like(total))
        h_ref[slot] = acc[:, sl] * r * jnp.float32(ROWS)


def late_product(meta, keep, slots, inv, early, a_pieces, b_pieces):
    anywhere = pl.BlockSpec(memory_space=pltpu.HBM)
    smem = pl.BlockSpec(memory_space=pltpu.SMEM)
    vmem = pl.BlockSpec(memory_space=pltpu.VMEM)
    return pl.pallas_call(
        late_kernel,
        in_specs=[smem] * 3 + [vmem] * 4 + [anywhere] * 15,
        out_specs=[vmem] * 2,
        out_shape=[
            jax.ShapeDtypeStruct((NC * CAP, ROWS, BLK), jnp.float32),
            jax.ShapeDtypeStruct((NC * CAP, BLK), jnp.float32),
        ],
        scratch_shapes=[
            pltpu.VMEM((4, ROWS, COLS), jnp.bfloat16),
            pltpu.VMEM((4, 2 * ROWS, COLS), jnp.bfloat16),
            pltpu.VMEM((ROWS, COLS), jnp.float32),
            pltpu.SemaphoreType.DMA((16,)),
        ],
        compiler_params=pltpu.CompilerParams(vmem_limit_bytes=LATE_LIMIT),
    )(meta, keep, slots, inv, *early, *a_pieces, *b_pieces)


def columns_kernel(index, x_ref, o_ref, sem):
    copies = []
    for j in range(NC):
        dst = o_ref.at[:, pl.ds(j * BLK, BLK)]
        copies.append(pltpu.make_async_copy(x_ref.at[index[j]], dst, sem.at[j]))
    for copy in copies:
        copy.start()
    for copy in copies:
        copy.wait()


def side_by_side(index, blocks):
    return pl.pallas_call(
        columns_kernel,
        in_specs=[pl.BlockSpec(memory_space=pltpu.SMEM), pl.BlockSpec(memory_space=pltpu.VMEM)],
        out_specs=pl.BlockSpec(memory_space=pltpu.HBM),
        out_shape=jax.ShapeDtypeStruct((ROWS, COLS), jnp.float32),
        scratch_shapes=[pltpu.SemaphoreType.DMA((NC,))],
        compiler_params=pltpu.CompilerParams(vmem_limit_bytes=LAST_LIMIT),
    )(index, pltpu.with_memory_space_constraint(blocks, pltpu.VMEM))


def slot_tables(owners, me_col):
    table = owners.reshape(NC, NC)
    dest = table // NC
    earlier = jnp.arange(NC)[:, None] < jnp.arange(NC)[None, :]
    same = dest[:, :, None] == dest[:, None, :]
    rank = jnp.sum(jnp.where(same & earlier, 1, 0), axis=1)
    mine = lax.dynamic_slice(dest, (me_col, 0), (1, NC))[0]
    my_rank = lax.dynamic_slice(rank, (me_col, 0), (1, NC))[0]
    outgoing = mine * CAP + my_rank
    slot_of = jnp.arange(NC)[:, None] * CAP + rank
    wanted = me_col * NC + jnp.arange(NC)
    match = table[None] == wanted[:, None, None]
    incoming = jnp.sum(jnp.where(match, slot_of[None], 0), axis=(1, 2))
    return outgoing.astype(jnp.int32), incoming.astype(jnp.int32)


def body(values, pattern, pruning, owners):
    me_row = lax.axis_index("row").astype(jnp.int32)
    me_col = lax.axis_index("col").astype(jnp.int32)
    meta = jnp.stack([me_row >> 3, (me_row >> 1) & 3, me_row & 1, me_col >> 1, me_col & 1])
    nb = ROWS // BLK
    m, every = mask_and_sum((me_row * NC + me_col).reshape(1), pattern, values)

    core, ring_z, ring_y = flip("t"), spread("z"), spread("y")

    def swap(x):
        return send(x, core)

    keep = lax.dynamic_slice(pruning, (me_row * nb, me_col * NC), (nb, NC))
    keep = keep.reshape(nb * NC)
    outgoing, incoming = slot_tables(owners, me_col)
    yu = send(m, ring_y)
    mo = send(m, core)
    h = send(m, flip("xh"))
    zu = send(m, ring_z)
    d = jnp.sum(lax.all_to_all(every, "row", 0, 0, tiled=True), axis=0)
    yv = send(mo, ring_y)
    zv = send(mo, ring_z)
    fa = send(m[: ROWS // 2], flip("xl"))
    fb = send(m[ROWS // 2 :], flip("xl"))
    yuu = send(yu, ring_y)
    zuu = send(zu, ring_z)
    ho = send(h, core)
    yh = send(h, ring_y)
    yho = send(ho, ring_y)
    inv = jnp.broadcast_to((1.0 / d)[None], (NC, NC, BLK))
    inv = lax.all_to_all(inv, "col", 0, 0, tiled=True).reshape(NC, COLS)
    foa = send(fa, core)
    zfa = send(fa, ring_z)
    zfoa = send(foa, ring_z)
    xzz = send(zuu, flip("xl"))
    fob = send(fb, core)
    zfb = send(fb, ring_z)
    zfob = send(fob, ring_z)
    yhh = send(yh, ring_y)
    szfoa = send(zfoa, core)
    early = early_product(
        meta, (keep, outgoing, incoming), inv,
        [m, zu, swap(zv), zuu],
        [m, mo, yu, yv, swap(yv), swap(yu), yuu, swap(yuu)],
        [h, ho, yh, yho],
    )
    shares, sums = late_product(
        meta, keep, outgoing, inv, early,
        [fa, fb, zfa, zfb, szfoa, swap(zfob), xzz],
        [h, ho, yh, yho, swap(yho), swap(yh), yhh, swap(yhh)],
    )
    slots, sums = lax.optimization_barrier((shares.astype(jnp.float16), sums))
    sums = lax.all_to_all(sums, "col", 0, 0, tiled=True)
    arrived = lax.all_to_all(slots, "col", 0, 0, tiled=True)
    total = sums + send(sums, core)
    total = total + send(total, ring_xor(1))
    total = total + send(total, ring_xor(2))
    total = total + send(total, flip("xh"))
    weight = sums / total * jnp.float32(NR)
    placed = arrived.astype(jnp.float32) * weight[:, None, :]
    return side_by_side(incoming, placed)


def solution(mesh):
    return jax.shard_map(
        body,
        mesh=mesh,
        in_specs=(P("row", "col"), P(), P(), P()),
        out_specs=P("row", "col"),
        check_vma=False,
    )
```
